32 devices in a mesh: mem: 16 (over z, y, core), tile: 2 (over x).
Axes of the slice: x: 2, y: 2, z: 4, core: 2. Of those that a mesh axis runs over, the one named last changes fastest.
Arguments:
- member_perturbations: float32 [3, 32, 16, 256], P(None, 'mem', None, 'tile'), may hold values from -3 to 3
- obs_index: int32 [16, 2, 256], P('mem', 'tile'), may hold values from 0 to 383
- obs_value: float32 [16, 2, 256], P('mem', 'tile'), may hold values from -4 to 4
- obs_var: float32 [16, 2, 256], P('mem', 'tile'), may hold values from 0.05 to 0.5
- loc_weight: float32 [16, 2, 256], P('mem', 'tile'), may hold values from 0.2 to 1
Outputs:
- forecast: float32 [3, 32, 16, 256], P(None, 'mem', None, 'tile')
The draws below stay inside these ranges and needn't reach their ends.
All inputs are finite; a program needn't handle non-finite values.
Results may differ from the reference program's by a relative error of at most 0.0003.
Values sent between devices are 32-bit elements; how exact they have to be, the bound alone decides.
A program may use at most 64 MiB of HBM per device.

```python
import math
import jax
import jax.numpy as jnp
from jax import lax

PCELL = 128
NOBS = 256
STEPS = 1
NSIT = 6
MEM = 32
NY = 16
NX = 256


def touch_ends(array, rng, low, top_value):
    longest = array.shape.index(max(array.shape))
    spots = []
    for shift in (0, 1):
        where = [jax.random.randint(jax.random.fold_in(rng, axis), (), 0, length) for axis, length in enumerate(array.shape)]
        where[longest] = (where[longest] + shift) % array.shape[longest]
        spots.append(tuple(where))
    return array.at[spots[0]].set(low).at[spots[1]].set(top_value)


def shard_levels(stream_key, dims, pieces, low, top_value):
    loudness = 1.0
    for position, parts in pieces:
        draws = jax.random.uniform(jax.random.fold_in(jax.random.fold_in(stream_key, 6), position), (parts,), jnp.float32, low / len(pieces), top_value / len(pieces))
        loudness = loudness * jnp.repeat(jnp.exp(draws), dims[position] // parts).reshape((-1,) + (1,) * (len(dims) - 1 - position))
    return loudness


def normal_values(stream_key, dims, deviation, bound, cuts=(), kind=jnp.bfloat16):
    entries = jax.random.normal(stream_key, dims, jnp.float32) * deviation
    if len(cuts) > 0:
        entries = shard_levels(stream_key, dims, cuts, -0.22, 0.18) * entries
    return jnp.clip(entries, min=-bound, max=bound).astype(kind)


def setup_inputs(seed: int = 0) -> dict:
    key_of = jax.random.split(jax.random.key(seed), 6)
    return {
        "member_perturbations": normal_values(key_of[0], (3, MEM, NY, NX), 0.5, 3.0, ((1, 16), (3, 2)), jnp.float32),
        "obs_index": touch_ends(jax.random.randint(key_of[1], (NY, NX // PCELL, NOBS), 0, 3 * PCELL), jax.random.fold_in(key_of[1], 1), 0, (3 * PCELL) - 1).astype(jnp.int32),
        "obs_value": normal_values(key_of[2], (NY, NX // PCELL, NOBS), 1.0, 4.0, ((0, 16), (1, 2)), jnp.float32),
        "obs_var": jnp.clip(jnp.exp(math.log(0.5) - 2.3025851 * jax.random.uniform(key_of[3], (NY, NX // PCELL, NOBS), jnp.float32) ** shard_levels(key_of[3], (NY, NX // PCELL, NOBS), ((0, 16), (1, 2)), -0.2, 0.2)), 0.05, 0.5),
        "loc_weight": jnp.clip(0.2 + 0.8 * jax.random.uniform(key_of[4], (NY, NX // PCELL, NOBS), jnp.float32) ** shard_levels(key_of[4], (NY, NX // PCELL, NOBS), ((0, 16), (1, 2)), -0.2, 0.2), 0.2, 1.0),
    }


mean_depth = 4.0
gravity = 0.25
coriolis = 0.1
time_step = 0.3
highest = lax.Precision.HIGHEST

def across(field):
    return (jnp.roll(field, -1, -1) - jnp.roll(field, 1, -1)) * 0.5

def along(field):
    return (jnp.roll(field, -1, -2) - jnp.roll(field, 1, -2)) * 0.5

def tendency(dynamics_variables):
    height = dynamics_variables[0]
    east_wind = dynamics_variables[1]
    north_wind = dynamics_variables[2]
    depth_total = mean_depth + height
    d_height = -(across(depth_total * east_wind) + along(depth_total * north_wind))
    d_east = -(east_wind * across(east_wind) + north_wind * along(east_wind)) - gravity * across(height) + coriolis * north_wind
    d_north = -(east_wind * across(north_wind) + north_wind * along(north_wind)) - gravity * along(height) - coriolis * east_wind
    return jnp.stack([d_height, d_east, d_north])

def advance(dynamics_variables):
    for _ in range(STEPS):
        first_slope = tendency(dynamics_variables)
        slope_two = tendency(dynamics_variables + 0.5 * time_step * first_slope)
        slope_three = tendency(dynamics_variables + 0.5 * time_step * slope_two)
        slope_four = tendency(dynamics_variables + time_step * slope_three)
        dynamics_variables = dynamics_variables + time_step / 6.0 * (first_slope + 2.0 * slope_two + 2.0 * slope_three + slope_four)
    return dynamics_variables

def propagate_members_ahead(member_perturbations):
    members_first = jnp.moveaxis(member_perturbations, 1, 0)
    moved = lax.map(advance, members_first)
    return jnp.moveaxis(moved, 0, 1)

def product(left, right):
    return jnp.einsum('rbij,rbjk->rbik', left, right, precision=highest)

def analyse(blocks, indices, values, variances, locality):
    members = blocks.shape[1]
    row_count = blocks.shape[2]
    block_count = blocks.shape[3]
    cells = blocks.shape[4]
    xbar = lax.optimization_barrier(jnp.mean(blocks, axis=1, keepdims=True))
    pert = blocks - xbar
    flat = jnp.transpose(blocks, (2, 3, 0, 4, 1)).reshape(row_count, block_count, 3 * cells, members)
    observed = jnp.take_along_axis(flat, indices.astype(jnp.int32)[..., None], axis=2)
    ybar = lax.optimization_barrier(jnp.mean(observed, axis=3, keepdims=True))
    obs_pert = observed - ybar
    weighted = obs_pert * (locality / variances)[..., None]
    gram = jnp.einsum('rboi,rboj->rbij', weighted, obs_pert, precision=highest)
    identity = jnp.eye(members, dtype=jnp.float32)
    amat = gram + (members - 1.0) * identity
    frob = jnp.sqrt(lax.optimization_barrier(jnp.sum(amat * amat, axis=(2, 3), keepdims=True)))
    ymat = amat / frob
    zmat = jnp.broadcast_to(identity, amat.shape)
    for _ in range(NSIT):
        newton = 1.5 * identity - 0.5 * product(zmat, ymat)
        ymat = product(ymat, newton)
        zmat = product(newton, zmat)
    prec = product(zmat, zmat) / frob
    wmat = jnp.sqrt((members - 1.0) / frob) * zmat
    innov = values - ybar[..., 0]
    projected = jnp.einsum('rbok,rbo->rbk', weighted, innov, precision=highest)
    wbar = jnp.einsum('rbij,rbj->rbi', prec, projected, precision=highest)
    wtot = wmat + wbar[..., None]
    return xbar + jnp.einsum('virbc,rbij->vjrbc', pert, wtot, precision=highest)

def reference(member_perturbations, obs_index, obs_value, obs_var, loc_weight):
    background_member_set = propagate_members_ahead(member_perturbations)
    by_row = jnp.moveaxis(background_member_set, 2, 0)

    def one_row(inputs):
        row_fields, indices, values_row, var_row, loc_row = inputs
        members = row_fields.shape[1]
        blocks = row_fields.reshape(3, members, 1, NX // PCELL, PCELL)
        result = analyse(blocks, indices[None], values_row[None], var_row[None], loc_row[None])
        return result.reshape(3, members, NX)
    updated_member_set = lax.map(one_row, (by_row, obs_index, obs_value, obs_var, loc_weight))
    return propagate_members_ahead(jnp.moveaxis(updated_member_set, 0, 2))
```

```python
import functools

import jax
import jax.numpy as jnp
from jax import lax
from jax.experimental import pallas as pl
from jax.experimental.pallas import tpu as pltpu
from jax.sharding import PartitionSpec as P

PCELL = 128
NSIT = 6
HALO = 4

mean_depth = 4.0
gravity = 0.25
coriolis = 0.1
time_step = 0.3

MESH = pl.DeviceIdType.MESH
PAIRS = ((0, 0), (0, 1), (0, 2), (1, 0), (1, 1), (1, 2), (2, 0), (2, 1))


def across(field):
    width = field.shape[1]
    return (pltpu.roll(field, width - 1, 1) - pltpu.roll(field, 1, 1)) * 0.5


def along(field):
    rows = field.shape[0]
    return (pltpu.roll(field, rows - 1, 0) - pltpu.roll(field, 1, 0)) * 0.5


def tendency(fields):
    height, east, north = fields
    depth_total = mean_depth + height
    d_height = -(across(depth_total * east) + along(depth_total * north))
    d_east = -(east * across(east) + north * along(east)) - gravity * across(height) + coriolis * north
    d_north = -(east * across(north) + north * along(north)) - gravity * along(height) - coriolis * east
    return d_height, d_east, d_north


def advance(fields):
    def moved(scale, slopes):
        return [f + scale * s for f, s in zip(fields, slopes)]

    one = tendency(fields)
    two = tendency(moved(0.5 * time_step, one))
    total = [a + 2.0 * b for a, b in zip(one, two)]
    three = tendency(moved(0.5 * time_step, two))
    total = [a + 2.0 * b for a, b in zip(total, three)]
    four = tendency(moved(time_step, three))
    return [f + (time_step / 6.0) * (a + b) for f, a, b in zip(fields, total, four)]


def pieces(value):
    parts = []
    for _ in range(3):
        part = value.astype(jnp.bfloat16)
        parts.append(part)
        value = value - part.astype(jnp.float32)
    return parts


def left_factor(value, size):
    rep = 128 // size
    parts = [p.astype(jnp.float32) for p in pieces(value)]
    group = lax.broadcasted_iota(jnp.int32, value.shape, 1) // size
    tiles = []
    for first in range(0, len(PAIRS), rep):
        chosen = [parts[a] for a, _ in PAIRS[first : first + rep]]
        chosen += [jnp.zeros_like(value)] * (rep - len(chosen))
        tile = chosen[-1]
        for g in range(rep - 2, -1, -1):
            if chosen[g] is not chosen[g + 1]:
                tile = jnp.where(group <= g, chosen[g], tile)
        tiles.append(tile.astype(jnp.bfloat16))
    return jnp.concatenate(tiles, axis=1)


def right_factor(value, size):
    rep = 128 // size
    parts = pieces(value)
    stack = [parts[b] for _, b in PAIRS]
    stack += [parts[0]] * (-len(PAIRS) % rep)
    return jnp.concatenate(stack, axis=0)


def dot(left, right):
    return jnp.dot(left, right, preferred_element_type=jnp.float32)


def kernel(
    n, tiles, offsets, slot,
    x_hbm, idx_hbm, val_hbm, var_hbm, loc_hbm, out_ref,
    x, idx, val, var, loc, hs1, hr1, s1, r1, s2, r2, hs2, hr2,
    in_sem, hs1_sem, hr1_sem, s1_sem, r1_sem, s2_sem, r2_sem, hs2_sem, hr2_sem,
):
    me = lax.axis_index("mem")
    mt = lax.axis_index("tile")
    _, local, rows, width = x.shape
    members = n * local
    per_row = rows // 8

    loads = [
        pltpu.make_async_copy(src, dst, in_sem.at[i])
        for i, (src, dst) in enumerate(
            ((x_hbm, x), (idx_hbm, idx), (val_hbm, val), (var_hbm, var), (loc_hbm, loc))
        )
    ]
    for load in loads:
        load.start()

    def peers(body):
        def step(i, carry):
            body(lax.rem(me + i, n))
            return carry

        lax.fori_loop(1, n, step, 0, unroll=n <= 16)

    barrier = pltpu.get_barrier_semaphore()
    neighbours = [lax.rem(mt + d, tiles) for d in offsets]
    for t in neighbours:
        pl.semaphore_signal(barrier, inc=1, device_id=(me, t), device_id_type=MESH)
    peers(lambda p: pl.semaphore_signal(barrier, inc=1, device_id=(p, mt), device_id_type=MESH))

    lane = lax.broadcasted_iota(jnp.int32, (8, 128), 1)
    lane_rows = lax.broadcasted_iota(jnp.int32, (rows, 128), 1)
    lane_n = lax.broadcasted_iota(jnp.int32, (n, 128), 1)

    loads[0].wait()
    chunks = [(v, m, r) for v in range(3) for m in range(local) for r in range(per_row)]
    for block in range(hs1.shape[0]):
        packed = jnp.zeros((8, 128), jnp.float32)
        for g, (v, m, r) in enumerate(chunks[block * 16 : block * 16 + 16]):
            rolled = pltpu.roll(x[v, m, r * 8 : r * 8 + 8, :], (HALO + 8 * g) % 128, 1)
            packed = jnp.where((lane >= 8 * g) & (lane < 8 * g + 8), rolled, packed)
        hs1[block] = packed

    pl.semaphore_wait(barrier, n - 1 + len(offsets))

    halo_copies = [
        pltpu.make_async_remote_copy(
            src_ref=hs1, dst_ref=hr1.at[i], send_sem=hs1_sem.at[i], recv_sem=hr1_sem.at[i],
            device_id=(me, t), device_id_type=MESH,
        )
        for i, t in enumerate(neighbours)
    ]
    for copy in halo_copies:
        copy.start()

    for load in loads[1:]:
        load.wait()
    nobs = idx.shape[2]
    which = idx[0]
    entry = lax.broadcasted_iota(jnp.int32, (3 * PCELL, nobs), 0)
    picks = jnp.where(entry == which, 1.0, 0.0).astype(jnp.bfloat16)
    weight = loc[0] / var[0]

    for copy in halo_copies:
        copy.wait_recv()

    def edge_tile(sources, g, mask_lane):
        shift = (128 - HALO - 8 * g) % 128
        if len(sources) == 1:
            rolled = pltpu.roll(sources[0], shift, 1)
            return jnp.where((mask_lane < HALO) | (mask_lane >= 128 - HALO), rolled, 0.0)
        left = pltpu.roll(sources[0], shift, 1)
        right = pltpu.roll(sources[1], shift, 1)
        return jnp.where(mask_lane < HALO, right, jnp.where(mask_lane >= 128 - HALO, left, 0.0))

    for m in range(local):
        fields = []
        for v in range(3):
            edges = []
            for r in range(per_row):
                c = (v * local + m) * per_row + r
                sources = [hr1[i, c // 16] for i in range(len(offsets))]
                edges.append(edge_tile(sources, c % 16, lane))
            edge = edges[0] if per_row == 1 else jnp.concatenate(edges, axis=0)
            fields.append(jnp.concatenate([x[v, m], edge], axis=1))
        for v, field in enumerate(advance(fields)):
            s1[pl.ds(v * local + m, rows, stride=slot), :] = field[:, :128]

    def at_slot(ref, p):
        return ref.at[pl.ds(pl.multiple_of(p * slot, 8), slot), :]

    def own(source, target):
        where = pl.ds(pl.multiple_of(me * slot, 8), slot)
        target[where, :] = source[where, :]

    def row_copy(p, source, target, send_sem, recv_sem):
        return pltpu.make_async_remote_copy(
            src_ref=at_slot(source, p), dst_ref=at_slot(target, me),
            send_sem=send_sem, recv_sem=recv_sem, device_id=(p, mt), device_id_type=MESH,
        )

    def wait_slots(ref, sem):
        part = ref.at[pl.ds(0, (n - 1) * slot), :]
        pltpu.make_async_copy(part, part, sem).wait()

    peers(lambda p: row_copy(p, s1, r1, s1_sem, r1_sem).start())
    own(s1, r1)
    wait_slots(r1, r1_sem)

    state = jnp.concatenate(
        [
            jnp.concatenate([r1[pl.ds(v * local + m, n, stride=slot), :] for m in range(local)], axis=0)
            for v in range(3)
        ],
        axis=1,
    )
    seen = dot(jnp.concatenate(pieces(state), axis=0), picks)
    seen = seen[:members] + (seen[members : 2 * members] + seen[2 * members :])
    ybar = jnp.mean(seen, axis=0, keepdims=True)
    yp = seen - ybar
    yr = yp * weight
    rep = 128 // members
    yp_parts = [jnp.concatenate([p] * rep, axis=0) for p in pieces(yp)]
    yr_parts = pieces(yr)
    gram = None
    for b in (2, 1, 0):
        lefts = yr_parts[: 3 - b]
        left = lefts[0] if len(lefts) == 1 else jnp.concatenate(lefts, axis=0)
        full = lax.dot_general(
            left, yp_parts[b], (((1,), (1,)), ((), ())), preferred_element_type=jnp.float32
        )
        for a in range(len(lefts) - 1, -1, -1):
            part = full[a * members : (a + 1) * members]
            gram = part if gram is None else gram + part
    row_id = lax.broadcasted_iota(jnp.int32, (members, 128), 0)
    col_id = lax.rem(lax.broadcasted_iota(jnp.int32, (members, 128), 1), members)
    identity = jnp.where(row_id == col_id, 1.0, 0.0)
    amat = gram + (members - 1.0) * identity
    square = jnp.sum(jnp.sum(amat * amat, axis=0, keepdims=True), axis=1, keepdims=True)
    frob = jnp.sqrt(square * (1.0 / rep))
    inverse = 1.0 / frob

    xbar = jnp.mean(state, axis=0, keepdims=True)
    pert = state - xbar
    innov = val[0] - ybar
    projected = jnp.sum(yr * innov, axis=1, keepdims=True)
    carried = jnp.concatenate([pert, jnp.broadcast_to(projected, (members, 128))], axis=1)

    ymat = amat * inverse
    newton = 1.5 * identity - 0.5 * ymat
    ymat = dot(left_factor(newton, members), right_factor(ymat, members))
    zmat = newton
    for step in range(1, NSIT):
        zleft = left_factor(zmat, members)
        newton = 1.5 * identity - 0.5 * dot(zleft, right_factor(ymat, members))
        nleft = left_factor(newton, members)
        if step < NSIT - 1:
            both = dot(nleft, right_factor(jnp.concatenate([ymat, zmat], axis=1), members))
            ymat, zmat = both[:, :128], both[:, 128:]
        else:
            carried = dot(zleft, right_factor(carried, members))
            carried = dot(nleft, right_factor(carried, members))
    moved = carried[:, : 3 * PCELL]
    gain = carried[:, 3 * PCELL : 3 * PCELL + 1]
    shift = xbar + jnp.sum(moved * gain, axis=0, keepdims=True) * inverse
    updated = shift + jnp.sqrt((members - 1.0) * inverse) * moved

    packed = jnp.zeros((n, 128), jnp.float32)
    for v in range(3):
        for m in range(local):
            part = updated[m * n : (m + 1) * n, v * PCELL : (v + 1) * PCELL]
            k = v * local + m
            s2[pl.ds(k, n, stride=slot), :] = part
            rolled = pltpu.roll(part, (HALO + 8 * k) % 128, 1)
            packed = jnp.where((lane_n >= 8 * k) & (lane_n < 8 * k + 8), rolled, packed)
    for p in range(n):
        hs2[p] = packed[p : p + 1]

    def edge_copy(p, i):
        return pltpu.make_async_remote_copy(
            src_ref=hs2.at[p], dst_ref=hr2.at[i, me], send_sem=hs2_sem.at[i], recv_sem=hr2_sem.at[i],
            device_id=(p, neighbours[i]), device_id_type=MESH,
        )

    for i in range(len(offsets)):
        peers(lambda p: edge_copy(p, i).start())
        edge_copy(me, i).start()
    peers(lambda p: row_copy(p, s2, r2, s2_sem, r2_sem).start())
    own(s2, r2)

    for copy in halo_copies:
        copy.wait_send()
    wait_slots(s1, s1_sem)

    wait_slots(r2, r2_sem)
    for i in range(len(offsets)):
        pltpu.make_async_copy(hr2.at[i], hr2.at[i], hr2_sem.at[i]).wait()
    sources = [
        jnp.concatenate([hr2[i, r] for r in range(rows)], axis=0) for i in range(len(offsets))
    ]
    for m in range(local):
        fields = []
        for v in range(3):
            k = v * local + m
            edge = edge_tile(sources, k, lane_rows)
            fields.append(jnp.concatenate([r2[pl.ds(k, rows, stride=slot), :], edge], axis=1))
        for v, field in enumerate(advance(fields)):
            out_ref[v, m] = field[:, :128]

    wait_slots(s2, s2_sem)
    for i in range(len(offsets)):
        pltpu.make_async_copy(hs2, hs2, hs2_sem.at[i]).wait()


def local(n, tiles, member_perturbations, obs_index, obs_value, obs_var, loc_weight):
    x = member_perturbations
    _, count, rows, width = x.shape
    assert width == PCELL and rows == n and rows % 8 == 0
    assert obs_index.shape[:2] == (1, 1) and 128 % (n * count) == 0 and 24 * count <= 128
    slot = -(-3 * count // 8) * 8
    offsets = (1,) if tiles == 2 else (1, tiles - 1)
    blocks = -(-3 * count * (rows // 8) // 16)
    obs = obs_index.shape
    f32 = jnp.float32
    dma = pltpu.SemaphoreType.DMA
    sides = len(offsets)
    return pl.pallas_call(
        functools.partial(kernel, n, tiles, offsets, slot),
        out_shape=jax.ShapeDtypeStruct(x.shape, f32),
        in_specs=[pl.BlockSpec(memory_space=pl.ANY)] * 5,
        out_specs=pl.BlockSpec(memory_space=pltpu.VMEM),
        scratch_shapes=[
            pltpu.VMEM(x.shape, f32),
            pltpu.VMEM(obs, jnp.int32),
            pltpu.VMEM(obs, f32),
            pltpu.VMEM(obs, f32),
            pltpu.VMEM(obs, f32),
            pltpu.VMEM((blocks, 8, 128), f32),
            pltpu.VMEM((sides, blocks, 8, 128), f32),
            pltpu.VMEM((rows * slot, 128), f32),
            pltpu.VMEM((n * slot, 128), f32),
            pltpu.VMEM((n * slot, 128), f32),
            pltpu.VMEM((rows * slot, 128), f32),
            pltpu.VMEM((n, 1, 128), f32),
            pltpu.VMEM((sides, rows, 1, 128), f32),
            dma((5,)),
            dma((sides,)),
            dma((sides,)),
            dma,
            dma,
            dma,
            dma,
            dma((sides,)),
            dma((sides,)),
        ],
        compiler_params=pltpu.CompilerParams(collective_id=0, has_side_effects=True),
        name="cycle",
    )(x, obs_index, obs_value, obs_var, loc_weight)


def solution(mesh):
    in_specs = (
        P(None, "mem", None, "tile"),
        P("mem", "tile", None),
        P("mem", "tile", None),
        P("mem", "tile", None),
        P("mem", "tile", None),
    )
    out_specs = P(None, "mem", None, "tile")
    body = functools.partial(local, mesh.shape["mem"], mesh.shape["tile"])
    return jax.shard_map(body, mesh=mesh, in_specs=in_specs, out_specs=out_specs, check_vma=False)
```

```python
import functools

import jax
import jax.numpy as jnp
from jax import lax
from jax.experimental import pallas as pl
from jax.experimental.pallas import tpu as pltpu
from jax.sharding import PartitionSpec as P

PCELL = 128
NSIT = 6
HALO = 4

mean_depth = 4.0
gravity = 0.25
coriolis = 0.1
time_step = 0.3

MESH = pl.DeviceIdType.MESH
PAIRS = ((0, 0), (0, 1), (0, 2), (1, 0), (1, 1), (1, 2), (2, 0), (2, 1))


def across(field):
    width = field.shape[1]
    return (pltpu.roll(field, width - 1, 1) - pltpu.roll(field, 1, 1)) * 0.5


def along(field):
    rows = field.shape[0]
    return (pltpu.roll(field, rows - 1, 0) - pltpu.roll(field, 1, 0)) * 0.5


def tendency(fields):
    height, east, north = fields
    depth_total = mean_depth + height
    d_height = -(across(depth_total * east) + along(depth_total * north))
    d_east = -(east * across(east) + north * along(east)) - gravity * across(height) + coriolis * north
    d_north = -(east * across(north) + north * along(north)) - gravity * along(height) - coriolis * east
    return d_height, d_east, d_north


def advance(fields):
    def moved(scale, slopes):
        return [f + scale * s for f, s in zip(fields, slopes)]

    one = tendency(fields)
    two = tendency(moved(0.5 * time_step, one))
    total = [a + 2.0 * b for a, b in zip(one, two)]
    three = tendency(moved(0.5 * time_step, two))
    total = [a + 2.0 * b for a, b in zip(total, three)]
    four = tendency(moved(time_step, three))
    return [f + (time_step / 6.0) * (a + b) for f, a, b in zip(fields, total, four)]


def pieces(value):
    parts = []
    for _ in range(3):
        part = value.astype(jnp.bfloat16)
        parts.append(part)
        value = value - part.astype(jnp.float32)
    return parts


def left_factor(value, size):
    rep = 128 // size
    parts = [p.astype(jnp.float32) for p in pieces(value)]
    group = lax.broadcasted_iota(jnp.int32, value.shape, 1) // size
    tiles = []
    for first in range(0, len(PAIRS), rep):
        chosen = [parts[a] for a, _ in PAIRS[first : first + rep]]
        chosen += [jnp.zeros_like(value)] * (rep - len(chosen))
        tile = chosen[-1]
        for g in range(rep - 2, -1, -1):
            if chosen[g] is not chosen[g + 1]:
                tile = jnp.where(group <= g, chosen[g], tile)
        tiles.append(tile.astype(jnp.bfloat16))
    return jnp.concatenate(tiles, axis=1)


def right_factor(value, size):
    rep = 128 // size
    parts = pieces(value)
    stack = [parts[b] for _, b in PAIRS]
    stack += [parts[0]] * (-len(PAIRS) % rep)
    return jnp.concatenate(stack, axis=0)


def dot(left, right):
    return jnp.dot(left, right, preferred_element_type=jnp.float32)


def kernel(
    n, tiles, offsets, slot,
    x_hbm, idx_hbm, val_hbm, var_hbm, loc_hbm, out_ref,
    x, idx, val, var, loc, hs1, hr1, s1, r1, s2, r2, hs2, hr2,
    in_sem, hs1_sem, hr1_sem, s1_sem, r1_sem, s2_sem, r2_sem, hs2_sem, hr2_sem, told_sem,
):
    me = lax.axis_index("mem")
    mt = lax.axis_index("tile")
    _, local, rows, width = x.shape
    members = n * local
    per_row = rows // 8

    loads = [
        pltpu.make_async_copy(src, dst, in_sem.at[i])
        for i, (src, dst) in enumerate(
            ((x_hbm, x), (idx_hbm, idx), (val_hbm, val), (var_hbm, var), (loc_hbm, loc))
        )
    ]
    for load in loads:
        load.start()

    def peers(body):
        def step(i, carry):
            body(lax.rem(me + i, n))
            return carry

        lax.fori_loop(1, n, step, 0, unroll=n <= 16)

    barrier = pltpu.get_barrier_semaphore()
    neighbours = [lax.rem(mt + d, tiles) for d in offsets]
    odd = lax.rem(me, 2)
    even_one = me - odd
    partner = me + 1 - 2 * odd
    for t in neighbours:
        pl.semaphore_signal(barrier, inc=1, device_id=(even_one, t), device_id_type=MESH)

    pl.semaphore_signal(barrier, inc=1, device_id=(partner, mt), device_id_type=MESH)

    def greet(i, carry):
        p = lax.rem(even_one + 2 * i, n) + 1
        pl.semaphore_signal(barrier, inc=1, device_id=(p, mt), device_id_type=MESH)
        return carry

    lax.fori_loop(1, n // 2, greet, 0, unroll=n <= 16)

    lane = lax.broadcasted_iota(jnp.int32, (8, 128), 1)
    lane_rows = lax.broadcasted_iota(jnp.int32, (rows, 128), 1)
    lane_n = lax.broadcasted_iota(jnp.int32, (n, 128), 1)

    loads[0].wait()
    chunks = [(v, m, r) for v in range(3) for m in range(local) for r in range(per_row)]
    for block in range(hs1.shape[0]):
        packed = jnp.zeros((8, 128), jnp.float32)
        for g, (v, m, r) in enumerate(chunks[block * 16 : block * 16 + 16]):
            rolled = pltpu.roll(x[v, m, r * 8 : r * 8 + 8, :], (HALO + 8 * g) % 128, 1)
            packed = jnp.where((lane >= 8 * g) & (lane < 8 * g + 8), rolled, packed)
        hs1[block] = packed

    @pl.when(odd == 0)
    def _():
        pl.semaphore_wait(barrier, 1 + 2 * len(offsets))
        pl.semaphore_signal(told_sem, inc=1, device_id=(partner, mt), device_id_type=MESH)

    @pl.when(odd == 1)
    def _():
        pl.semaphore_wait(told_sem, 1)

    halo_copies = [
        pltpu.make_async_remote_copy(
            src_ref=hs1, dst_ref=hr1.at[i], send_sem=hs1_sem.at[i], recv_sem=hr1_sem.at[i],
            device_id=(me, t), device_id_type=MESH,
        )
        for i, t in enumerate(neighbours)
    ]
    for copy in halo_copies:
        copy.start()

    for load in loads[1:]:
        load.wait()
    nobs = idx.shape[2]
    which = idx[0]
    entry = lax.broadcasted_iota(jnp.int32, (3 * PCELL, nobs), 0)
    picks = jnp.where(entry == which, 1.0, 0.0).astype(jnp.bfloat16)
    weight = loc[0] / var[0]

    for copy in halo_copies:
        copy.wait_recv()

    def edge_tile(sources, g, mask_lane):
        shift = (128 - HALO - 8 * g) % 128
        if len(sources) == 1:
            rolled = pltpu.roll(sources[0], shift, 1)
            return jnp.where((mask_lane < HALO) | (mask_lane >= 128 - HALO), rolled, 0.0)
        left = pltpu.roll(sources[0], shift, 1)
        right = pltpu.roll(sources[1], shift, 1)
        return jnp.where(mask_lane < HALO, right, jnp.where(mask_lane >= 128 - HALO, left, 0.0))

    for m in range(local):
        fields = []
        for v in range(3):
            edges = []
            for r in range(per_row):
                c = (v * local + m) * per_row + r
                sources = [hr1[i, c // 16] for i in range(len(offsets))]
                edges.append(edge_tile(sources, c % 16, lane))
            edge = edges[0] if per_row == 1 else jnp.concatenate(edges, axis=0)
            fields.append(jnp.concatenate([x[v, m], edge], axis=1))
        for v, field in enumerate(advance(fields)):
            s1[pl.ds(v * local + m, rows, stride=slot), :] = field[:, :128]

    def at_slot(ref, p):
        return ref.at[pl.ds(pl.multiple_of(p * slot, 8), slot), :]

    def own(source, target):
        where = pl.ds(pl.multiple_of(me * slot, 8), slot)
        target[where, :] = source[where, :]

    def row_copy(p, source, target, send_sem, recv_sem):
        return pltpu.make_async_remote_copy(
            src_ref=at_slot(source, p), dst_ref=at_slot(target, me),
            send_sem=send_sem, recv_sem=recv_sem, device_id=(p, mt), device_id_type=MESH,
        )

    def wait_slots(ref, sem):
        part = ref.at[pl.ds(0, (n - 1) * slot), :]
        pltpu.make_async_copy(part, part, sem).wait()

    @pl.when(odd == 1)
    def _():
        pl.semaphore_wait(barrier, n - 1)
        pl.semaphore_signal(told_sem, inc=1, device_id=(partner, mt), device_id_type=MESH)

    @pl.when(odd == 0)
    def _():
        pl.semaphore_wait(told_sem, 1)

    peers(lambda p: row_copy(p, s1, r1, s1_sem, r1_sem).start())
    own(s1, r1)
    wait_slots(r1, r1_sem)

    state = jnp.concatenate(
        [
            jnp.concatenate([r1[pl.ds(v * local + m, n, stride=slot), :] for m in range(local)], axis=0)
            for v in range(3)
        ],
        axis=1,
    )
    seen = dot(jnp.concatenate(pieces(state), axis=0), picks)
    seen = seen[:members] + (seen[members : 2 * members] + seen[2 * members :])
    ybar = jnp.mean(seen, axis=0, keepdims=True)
    yp = seen - ybar
    yr = yp * weight
    rep = 128 // members
    yp_parts = [jnp.concatenate([p] * rep, axis=0) for p in pieces(yp)]
    yr_parts = pieces(yr)
    gram = None
    for b in (2, 1, 0):
        lefts = yr_parts[: 3 - b]
        left = lefts[0] if len(lefts) == 1 else jnp.concatenate(lefts, axis=0)
        full = lax.dot_general(
            left, yp_parts[b], (((1,), (1,)), ((), ())), preferred_element_type=jnp.float32
        )
        for a in range(len(lefts) - 1, -1, -1):
            part = full[a * members : (a + 1) * members]
            gram = part if gram is None else gram + part
    row_id = lax.broadcasted_iota(jnp.int32, (members, 128), 0)
    col_id = lax.rem(lax.broadcasted_iota(jnp.int32, (members, 128), 1), members)
    identity = jnp.where(row_id == col_id, 1.0, 0.0)
    amat = gram + (members - 1.0) * identity
    square = jnp.sum(jnp.sum(amat * amat, axis=0, keepdims=True), axis=1, keepdims=True)
    frob = jnp.sqrt(square * (1.0 / rep))
    inverse = 1.0 / frob

    xbar = jnp.mean(state, axis=0, keepdims=True)
    pert = state - xbar
    innov = val[0] - ybar
    projected = jnp.sum(yr * innov, axis=1, keepdims=True)
    carried = jnp.concatenate([pert, jnp.broadcast_to(projected, (members, 128))], axis=1)

    ymat = amat * inverse
    newton = 1.5 * identity - 0.5 * ymat
    ymat = dot(left_factor(newton, members), right_factor(ymat, members))
    zmat = newton
    for step in range(1, NSIT):
        zleft = left_factor(zmat, members)
        newton = 1.5 * identity - 0.5 * dot(zleft, right_factor(ymat, members))
        nleft = left_factor(newton, members)
        if step < NSIT - 1:
            both = dot(nleft, right_factor(jnp.concatenate([ymat, zmat], axis=1), members))
            ymat, zmat = both[:, :128], both[:, 128:]
        else:
            carried = dot(zleft, right_factor(carried, members))
            carried = dot(nleft, right_factor(carried, members))
    moved = carried[:, : 3 * PCELL]
    gain = carried[:, 3 * PCELL : 3 * PCELL + 1]
    shift = xbar + jnp.sum(moved * gain, axis=0, keepdims=True) * inverse
    updated = shift + jnp.sqrt((members - 1.0) * inverse) * moved

    packed = jnp.zeros((n, 128), jnp.float32)
    for v in range(3):
        for m in range(local):
            part = updated[m * n : (m + 1) * n, v * PCELL : (v + 1) * PCELL]
            k = v * local + m
            s2[pl.ds(k, n, stride=slot), :] = part
            rolled = pltpu.roll(part, (HALO + 8 * k) % 128, 1)
            packed = jnp.where((lane_n >= 8 * k) & (lane_n < 8 * k + 8), rolled, packed)
    for p in range(n):
        hs2[p] = packed[p : p + 1]

    def edge_copy(p, i):
        return pltpu.make_async_remote_copy(
            src_ref=hs2.at[p], dst_ref=hr2.at[i, me], send_sem=hs2_sem.at[i], recv_sem=hr2_sem.at[i],
            device_id=(p, neighbours[i]), device_id_type=MESH,
        )

    for i in range(len(offsets)):
        peers(lambda p: edge_copy(p, i).start())
        edge_copy(me, i).start()
    peers(lambda p: row_copy(p, s2, r2, s2_sem, r2_sem).start())
    own(s2, r2)

    for copy in halo_copies:
        copy.wait_send()
    wait_slots(s1, s1_sem)

    wait_slots(r2, r2_sem)
    for i in range(len(offsets)):
        pltpu.make_async_copy(hr2.at[i], hr2.at[i], hr2_sem.at[i]).wait()
    sources = [
        jnp.concatenate([hr2[i, r] for r in range(rows)], axis=0) for i in range(len(offsets))
    ]
    for m in range(local):
        fields = []
        for v in range(3):
            k = v * local + m
            edge = edge_tile(sources, k, lane_rows)
            fields.append(jnp.concatenate([r2[pl.ds(k, rows, stride=slot), :], edge], axis=1))
        for v, field in enumerate(advance(fields)):
            out_ref[v, m] = field[:, :128]

    wait_slots(s2, s2_sem)
    for i in range(len(offsets)):
        pltpu.make_async_copy(hs2, hs2, hs2_sem.at[i]).wait()


def local(n, tiles, member_perturbations, obs_index, obs_value, obs_var, loc_weight):
    x = member_perturbations
    _, count, rows, width = x.shape
    assert width == PCELL and rows == n and rows % 8 == 0 and n % 2 == 0
    assert obs_index.shape[:2] == (1, 1) and 128 % (n * count) == 0 and 24 * count <= 128
    slot = -(-3 * count // 8) * 8
    offsets = (1,) if tiles == 2 else (1, tiles - 1)
    blocks = -(-3 * count * (rows // 8) // 16)
    obs = obs_index.shape
    f32 = jnp.float32
    dma = pltpu.SemaphoreType.DMA
    sides = len(offsets)
    return pl.pallas_call(
        functools.partial(kernel, n, tiles, offsets, slot),
        out_shape=jax.ShapeDtypeStruct(x.shape, f32),
        in_specs=[pl.BlockSpec(memory_space=pl.ANY)] * 5,
        out_specs=pl.BlockSpec(memory_space=pltpu.VMEM),
        scratch_shapes=[
            pltpu.VMEM(x.shape, f32),
            pltpu.VMEM(obs, jnp.int32),
            pltpu.VMEM(obs, f32),
            pltpu.VMEM(obs, f32),
            pltpu.VMEM(obs, f32),
            pltpu.VMEM((blocks, 8, 128), f32),
            pltpu.VMEM((sides, blocks, 8, 128), f32),
            pltpu.VMEM((rows * slot, 128), f32),
            pltpu.VMEM((n * slot, 128), f32),
            pltpu.VMEM((n * slot, 128), f32),
            pltpu.VMEM((rows * slot, 128), f32),
            pltpu.VMEM((n, 1, 128), f32),
            pltpu.VMEM((sides, rows, 1, 128), f32),
            dma((5,)),
            dma((sides,)),
            dma((sides,)),
            dma,
            dma,
            dma,
            dma,
            dma((sides,)),
            dma((sides,)),
            pltpu.SemaphoreType.REGULAR,
        ],
        compiler_params=pltpu.CompilerParams(collective_id=0, has_side_effects=True),
        name="cycle",
    )(x, obs_index, obs_value, obs_var, loc_weight)


def solution(mesh):
    in_specs = (
        P(None, "mem", None, "tile"),
        P("mem", "tile", None),
        P("mem", "tile", None),
        P("mem", "tile", None),
        P("mem", "tile", None),
    )
    out_specs = P(None, "mem", None, "tile")
    body = functools.partial(local, mesh.shape["mem"], mesh.shape["tile"])
    return jax.shard_map(body, mesh=mesh, in_specs=in_specs, out_specs=out_specs, check_vma=False)
```

```python
import functools

import jax
import jax.numpy as jnp
from jax import lax
from jax.experimental import pallas as pl
from jax.experimental.pallas import tpu as pltpu
from jax.sharding import PartitionSpec as P

PCELL = 128
NSIT = 6
HALO = 4

mean_depth = 4.0
gravity = 0.25
coriolis = 0.1
time_step = 0.3

MESH = pl.DeviceIdType.MESH
PAIRS = ((0, 0), (0, 1), (0, 2), (1, 0), (1, 1), (1, 2), (2, 0), (2, 1))


def across(field):
    width = field.shape[1]
    return (pltpu.roll(field, width - 1, 1) - pltpu.roll(field, 1, 1)) * 0.5


def along(field):
    rows = field.shape[0]
    return (pltpu.roll(field, rows - 1, 0) - pltpu.roll(field, 1, 0)) * 0.5


def tendency(fields):
    height, east, north = fields
    depth_total = mean_depth + height
    d_height = -(across(depth_total * east) + along(depth_total * north))
    d_east = -(east * across(east) + north * along(east)) - gravity * across(height) + coriolis * north
    d_north = -(east * across(north) + north * along(north)) - gravity * along(height) - coriolis * east
    return d_height, d_east, d_north


def advance(fields):
    def moved(scale, slopes):
        return [f + scale * s for f, s in zip(fields, slopes)]

    one = tendency(fields)
    two = tendency(moved(0.5 * time_step, one))
    total = [a + 2.0 * b for a, b in zip(one, two)]
    three = tendency(moved(0.5 * time_step, two))
    total = [a + 2.0 * b for a, b in zip(total, three)]
    four = tendency(moved(time_step, three))
    return [f + (time_step / 6.0) * (a + b) for f, a, b in zip(fields, total, four)]


def pieces(value):
    parts = []
    for _ in range(3):
        part = value.astype(jnp.bfloat16)
        parts.append(part)
        value = value - part.astype(jnp.float32)
    return parts


def left_factor(value, size):
    rep = 128 // size
    parts = [p.astype(jnp.float32) for p in pieces(value)]
    group = lax.broadcasted_iota(jnp.int32, value.shape, 1) // size
    tiles = []
    for first in range(0, len(PAIRS), rep):
        chosen = [parts[a] for a, _ in PAIRS[first : first + rep]]
        chosen += [jnp.zeros_like(value)] * (rep - len(chosen))
        tile = chosen[-1]
        for g in range(rep - 2, -1, -1):
            if chosen[g] is not chosen[g + 1]:
                tile = jnp.where(group <= g, chosen[g], tile)
        tiles.append(tile.astype(jnp.bfloat16))
    return jnp.concatenate(tiles, axis=1)


def right_factor(value, size):
    rep = 128 // size
    parts = pieces(value)
    stack = [parts[b] for _, b in PAIRS]
    stack += [parts[0]] * (-len(PAIRS) % rep)
    return jnp.concatenate(stack, axis=0)


def dot(left, right):
    return jnp.dot(left, right, preferred_element_type=jnp.float32)


def edge_tile(sources, g, mask_lane):
    shift = (128 - HALO - 8 * g) % 128
    if len(sources) == 1:
        rolled = pltpu.roll(sources[0], shift, 1)
        return jnp.where((mask_lane < HALO) | (mask_lane >= 128 - HALO), rolled, 0.0)
    left = pltpu.roll(sources[0], shift, 1)
    right = pltpu.roll(sources[1], shift, 1)
    return jnp.where(mask_lane < HALO, right, jnp.where(mask_lane >= 128 - HALO, left, 0.0))


def kernel(
    n, tiles, offsets, slot,
    x_hbm, idx_hbm, val_hbm, var_hbm, loc_hbm, r2, hr2,
    x, idx, val, var, loc, hs1, hr1, s1, r1, s2, hs2,
    in_sem, hs1_sem, hr1_sem, s1_sem, r1_sem, s2_sem, r2_sem, hs2_sem, hr2_sem, told_sem,
):
    me = lax.axis_index("mem")
    mt = lax.axis_index("tile")
    _, local, rows, width = x.shape
    members = n * local
    per_row = rows // 8

    loads = [
        pltpu.make_async_copy(src, dst, in_sem.at[i])
        for i, (src, dst) in enumerate(
            ((x_hbm, x), (idx_hbm, idx), (val_hbm, val), (var_hbm, var), (loc_hbm, loc))
        )
    ]
    for load in loads:
        load.start()

    def peers(body):
        def step(i, carry):
            body(lax.rem(me + i, n))
            return carry

        lax.fori_loop(1, n, step, 0, unroll=n <= 16)

    barrier = pltpu.get_barrier_semaphore()
    neighbours = [lax.rem(mt + d, tiles) for d in offsets]
    odd = lax.rem(me, 2)
    even_one = me - odd
    partner = me + 1 - 2 * odd
    for t in neighbours:
        pl.semaphore_signal(barrier, inc=1, device_id=(even_one, t), device_id_type=MESH)

    pl.semaphore_signal(barrier, inc=1, device_id=(partner, mt), device_id_type=MESH)

    def greet(i, carry):
        p = lax.rem(even_one + 2 * i, n) + 1
        pl.semaphore_signal(barrier, inc=1, device_id=(p, mt), device_id_type=MESH)
        return carry

    lax.fori_loop(1, n // 2, greet, 0, unroll=n <= 16)

    lane = lax.broadcasted_iota(jnp.int32, (8, 128), 1)
    lane_n = lax.broadcasted_iota(jnp.int32, (n, 128), 1)

    loads[0].wait()
    chunks = [(v, m, r) for v in range(3) for m in range(local) for r in range(per_row)]
    for block in range(hs1.shape[0]):
        packed = jnp.zeros((8, 128), jnp.float32)
        for g, (v, m, r) in enumerate(chunks[block * 16 : block * 16 + 16]):
            rolled = pltpu.roll(x[v, m, r * 8 : r * 8 + 8, :], (HALO + 8 * g) % 128, 1)
            packed = jnp.where((lane >= 8 * g) & (lane < 8 * g + 8), rolled, packed)
        hs1[block] = packed

    @pl.when(odd == 0)
    def _():
        pl.semaphore_wait(barrier, 1 + 2 * len(offsets))
        pl.semaphore_signal(told_sem, inc=1, device_id=(partner, mt), device_id_type=MESH)

    @pl.when(odd == 1)
    def _():
        pl.semaphore_wait(told_sem, 1)

    halo_copies = [
        pltpu.make_async_remote_copy(
            src_ref=hs1, dst_ref=hr1.at[i], send_sem=hs1_sem.at[i], recv_sem=hr1_sem.at[i],
            device_id=(me, t), device_id_type=MESH,
        )
        for i, t in enumerate(neighbours)
    ]
    for copy in halo_copies:
        copy.start()

    for load in loads[1:]:
        load.wait()
    nobs = idx.shape[2]
    which = idx[0]
    entry = lax.broadcasted_iota(jnp.int32, (3 * PCELL, nobs), 0)
    picks = jnp.where(entry == which, 1.0, 0.0).astype(jnp.bfloat16)
    weight = loc[0] / var[0]

    for copy in halo_copies:
        copy.wait_recv()

    for m in range(local):
        fields = []
        for v in range(3):
            edges = []
            for r in range(per_row):
                c = (v * local + m) * per_row + r
                sources = [hr1[i, c // 16] for i in range(len(offsets))]
                edges.append(edge_tile(sources, c % 16, lane))
            edge = edges[0] if per_row == 1 else jnp.concatenate(edges, axis=0)
            fields.append(jnp.concatenate([x[v, m], edge], axis=1))
        for v, field in enumerate(advance(fields)):
            s1[pl.ds(v * local + m, rows, stride=slot), :] = field[:, :128]

    def at_slot(ref, p):
        return ref.at[pl.ds(pl.multiple_of(p * slot, 8), slot), :]

    def own(source, target):
        where = pl.ds(pl.multiple_of(me * slot, 8), slot)
        target[where, :] = source[where, :]

    def row_copy(p, source, target, send_sem, recv_sem):
        return pltpu.make_async_remote_copy(
            src_ref=at_slot(source, p), dst_ref=at_slot(target, me),
            send_sem=send_sem, recv_sem=recv_sem, device_id=(p, mt), device_id_type=MESH,
        )

    def wait_slots(ref, sem):
        part = ref.at[pl.ds(0, (n - 1) * slot), :]
        pltpu.make_async_copy(part, part, sem).wait()

    @pl.when(odd == 1)
    def _():
        pl.semaphore_wait(barrier, n - 1)
        pl.semaphore_signal(told_sem, inc=1, device_id=(partner, mt), device_id_type=MESH)

    @pl.when(odd == 0)
    def _():
        pl.semaphore_wait(told_sem, 1)

    peers(lambda p: row_copy(p, s1, r1, s1_sem, r1_sem).start())
    own(s1, r1)
    wait_slots(r1, r1_sem)

    state = jnp.concatenate(
        [
            jnp.concatenate([r1[pl.ds(v * local + m, n, stride=slot), :] for m in range(local)], axis=0)
            for v in range(3)
        ],
        axis=1,
    )
    seen = dot(jnp.concatenate(pieces(state), axis=0), picks)
    seen = seen[:members] + (seen[members : 2 * members] + seen[2 * members :])
    ybar = jnp.mean(seen, axis=0, keepdims=True)
    yp = seen - ybar
    yr = yp * weight
    rep = 128 // members
    yp_parts = [jnp.concatenate([p] * rep, axis=0) for p in pieces(yp)]
    yr_parts = pieces(yr)
    gram = None
    for b in (2, 1, 0):
        lefts = yr_parts[: 3 - b]
        left = lefts[0] if len(lefts) == 1 else jnp.concatenate(lefts, axis=0)
        full = lax.dot_general(
            left, yp_parts[b], (((1,), (1,)), ((), ())), preferred_element_type=jnp.float32
        )
        for a in range(len(lefts) - 1, -1, -1):
            part = full[a * members : (a + 1) * members]
            gram = part if gram is None else gram + part
    row_id = lax.broadcasted_iota(jnp.int32, (members, 128), 0)
    col_id = lax.rem(lax.broadcasted_iota(jnp.int32, (members, 128), 1), members)
    identity = jnp.where(row_id == col_id, 1.0, 0.0)
    amat = gram + (members - 1.0) * identity
    square = jnp.sum(jnp.sum(amat * amat, axis=0, keepdims=True), axis=1, keepdims=True)
    frob = jnp.sqrt(square * (1.0 / rep))
    inverse = 1.0 / frob

    xbar = jnp.mean(state, axis=0, keepdims=True)
    pert = state - xbar
    innov = val[0] - ybar
    projected = jnp.sum(yr * innov, axis=1, keepdims=True)
    carried = jnp.concatenate([pert, jnp.broadcast_to(projected, (members, 128))], axis=1)

    ymat = amat * inverse
    newton = 1.5 * identity - 0.5 * ymat
    ymat = dot(left_factor(newton, members), right_factor(ymat, members))
    zmat = newton
    for step in range(1, NSIT):
        zleft = left_factor(zmat, members)
        newton = 1.5 * identity - 0.5 * dot(zleft, right_factor(ymat, members))
        nleft = left_factor(newton, members)
        if step < NSIT - 1:
            both = dot(nleft, right_factor(jnp.concatenate([ymat, zmat], axis=1), members))
            ymat, zmat = both[:, :128], both[:, 128:]
        else:
            carried = dot(zleft, right_factor(carried, members))
            carried = dot(nleft, right_factor(carried, members))
    moved = carried[:, : 3 * PCELL]
    gain = carried[:, 3 * PCELL : 3 * PCELL + 1]
    shift = xbar + jnp.sum(moved * gain, axis=0, keepdims=True) * inverse
    updated = shift + jnp.sqrt((members - 1.0) * inverse) * moved

    packed = jnp.zeros((n, 128), jnp.float32)
    for v in range(3):
        for m in range(local):
            part = updated[m * n : (m + 1) * n, v * PCELL : (v + 1) * PCELL]
            k = v * local + m
            s2[pl.ds(k, n, stride=slot), :] = part
            rolled = pltpu.roll(part, (HALO + 8 * k) % 128, 1)
            packed = jnp.where((lane_n >= 8 * k) & (lane_n < 8 * k + 8), rolled, packed)
    for p in range(n):
        hs2[p] = packed[p : p + 1]

    def edge_copy(p, i):
        return pltpu.make_async_remote_copy(
            src_ref=hs2.at[p], dst_ref=hr2.at[i, me], send_sem=hs2_sem.at[i], recv_sem=hr2_sem.at[i],
            device_id=(p, neighbours[i]), device_id_type=MESH,
        )

    for i in range(len(offsets)):
        peers(lambda p: edge_copy(p, i).start())
        edge_copy(me, i).start()
    peers(lambda p: row_copy(p, s2, r2, s2_sem, r2_sem).start())
    keep = pltpu.make_async_copy(at_slot(s2, me), at_slot(r2, me), in_sem.at[0])
    keep.start()

    for copy in halo_copies:
        copy.wait_send()
    wait_slots(s1, s1_sem)

    keep.wait()
    wait_slots(r2, r2_sem)
    for i in range(len(offsets)):
        pltpu.make_async_copy(hr2.at[i], hr2.at[i], hr2_sem.at[i]).wait()
    wait_slots(s2, s2_sem)
    for i in range(len(offsets)):
        pltpu.make_async_copy(hs2, hs2, hs2_sem.at[i]).wait()


def finish(slot, r2_hbm, hr2_hbm, out_hbm, r2, hr2, out, in_sem, out_sem):
    loads = [
        pltpu.make_async_copy(r2_hbm, r2, in_sem.at[0]),
        pltpu.make_async_copy(hr2_hbm, hr2, in_sem.at[1]),
    ]
    for load in loads:
        load.start()
    for load in loads:
        load.wait()
    _, local, rows, _ = out.shape
    lane_rows = lax.broadcasted_iota(jnp.int32, (rows, 128), 1)
    sources = [
        jnp.concatenate([hr2[i, r] for r in range(rows)], axis=0) for i in range(hr2.shape[0])
    ]
    stores = []
    for m in range(local):
        fields = []
        for v in range(3):
            k = v * local + m
            edge = edge_tile(sources, k, lane_rows)
            fields.append(jnp.concatenate([r2[pl.ds(k, rows, stride=slot), :], edge], axis=1))
        for v, field in enumerate(advance(fields)):
            out[v, m] = field[:, :128]
            stores.append(pltpu.make_async_copy(out.at[v, m], out_hbm.at[v, m], out_sem.at[m, v]))
            stores[-1].start()
    for store in stores:
        store.wait()


def local(n, tiles, member_perturbations, obs_index, obs_value, obs_var, loc_weight):
    x = member_perturbations
    _, count, rows, width = x.shape
    assert width == PCELL and rows == n and rows % 8 == 0 and n % 2 == 0
    assert obs_index.shape[:2] == (1, 1) and 128 % (n * count) == 0 and 24 * count <= 128
    slot = -(-3 * count // 8) * 8
    offsets = (1,) if tiles == 2 else (1, tiles - 1)
    blocks = -(-3 * count * (rows // 8) // 16)
    obs = obs_index.shape
    f32 = jnp.float32
    dma = pltpu.SemaphoreType.DMA
    sides = len(offsets)
    hbm = pl.BlockSpec(memory_space=pl.ANY)
    rows_back, edges_back = pl.pallas_call(
        functools.partial(kernel, n, tiles, offsets, slot),
        out_shape=(
            jax.ShapeDtypeStruct((rows * slot, 128), f32),
            jax.ShapeDtypeStruct((sides, rows, 1, 128), f32),
        ),
        in_specs=[hbm] * 5,
        out_specs=(hbm, hbm),
        scratch_shapes=[
            pltpu.VMEM(x.shape, f32),
            pltpu.VMEM(obs, jnp.int32),
            pltpu.VMEM(obs, f32),
            pltpu.VMEM(obs, f32),
            pltpu.VMEM(obs, f32),
            pltpu.VMEM((blocks, 8, 128), f32),
            pltpu.VMEM((sides, blocks, 8, 128), f32),
            pltpu.VMEM((rows * slot, 128), f32),
            pltpu.VMEM((n * slot, 128), f32),
            pltpu.VMEM((n * slot, 128), f32),
            pltpu.VMEM((n, 1, 128), f32),
            dma((5,)),
            dma((sides,)),
            dma((sides,)),
            dma,
            dma,
            dma,
            dma,
            dma((sides,)),
            dma((sides,)),
            pltpu.SemaphoreType.REGULAR,
        ],
        compiler_params=pltpu.CompilerParams(collective_id=0, has_side_effects=True),
        name="cycle",
    )(x, obs_index, obs_value, obs_var, loc_weight)
    return pl.pallas_call(
        functools.partial(finish, slot),
        out_shape=jax.ShapeDtypeStruct(x.shape, f32),
        in_specs=[hbm, hbm],
        out_specs=hbm,
        scratch_shapes=[
            pltpu.VMEM((rows * slot, 128), f32),
            pltpu.VMEM((sides, rows, 1, 128), f32),
            pltpu.VMEM(x.shape, f32),
            dma((2,)),
            dma((count, 3)),
        ],
        name="second_step",
    )(rows_back, edges_back)


def solution(mesh):
    in_specs = (
        P(None, "mem", None, "tile"),
        P("mem", "tile", None),
        P("mem", "tile", None),
        P("mem", "tile", None),
        P("mem", "tile", None),
    )
    out_specs = P(None, "mem", None, "tile")
    body = functools.partial(local, mesh.shape["mem"], mesh.shape["tile"])
    return jax.shard_map(body, mesh=mesh, in_specs=in_specs, out_specs=out_specs, check_vma=False)
```
